32 devices in a mesh: seq: 16 (over z, y, x), head: 2 (over core).
Axes of the slice: x: 2, y: 2, z: 4, core: 2. Of those that a mesh axis runs over, the one named last changes fastest.
Arguments:
- tokens: float32 [4096, 1024], P('seq'), may hold values from -6 to 6
- norm_gain: float32 [1024], replicated, may hold values from 0.5 to 1.5
- proj_inner: bfloat16 [1024, 2048], P(None, 'head'), may hold values from -0.1875 to 0.1875
- proj_gate: bfloat16 [1024, 2048], P(None, 'head'), may hold values from -0.1875 to 0.1875
- proj_step: bfloat16 [1024, 32], P(None, 'head'), may hold values from -0.1875 to 0.1875
- proj_state: bfloat16 [1024, 256], P(None, 'head'), may hold values from -0.1875 to 0.1875
- conv_inner: float32 [4, 2048], P(None, 'head'), may hold values from -3 to 3
- conv_state: float32 [4, 256], P(None, 'head'), may hold values from -3 to 3
- offset_inner: float32 [2048], P('head'), may hold values from -2.5 to 2.5
- offset_state: float32 [256], P('head'), may hold values from -2.5 to 2.5
- step_bias: float32 [32], P('head'), may hold values from -4 to -2
- decay_log: float32 [32], P('head')
- skip_gain: float32 [32], P('head'), may hold values from 0.5 to 1.5
- gate_gain: float32 [2048], P('head'), may hold values from 0.5 to 1.5
- proj_output: bfloat16 [1024, 2048], P(None, 'head'), may hold values from -0.125 to 0.125
- seq_start: int32 [16], P('seq'), may hold values from 0 to 3584, as said below
- cotangent: float32 [4096, 1024], P('seq'), may hold values from -6 to 6
Outputs:
- block_output: float32 [4096, 1024], P('seq')
- input_grad: float32 [4096, 1024], P('seq')
- norm_gain_grad: float32 [1024], P('seq')
- proj_inner_grad: float32 [1024, 2048], P('seq', 'head')
- proj_gate_grad: float32 [1024, 2048], P('seq', 'head')
- proj_step_grad: float32 [1024, 32], P('seq', 'head')
- proj_state_grad: float32 [1024, 256], P('seq', 'head')
- conv_inner_grad: float32 [4, 2048], P(None, 'head')
- conv_state_grad: float32 [4, 256], P(None, 'head')
- offset_inner_grad: float32 [2048], P('head')
- offset_state_grad: float32 [256], P('head')
- step_bias_grad: float32 [32], P('head')
- decay_log_grad: float32 [32], P('head')
- skip_gain_grad: float32 [32], P('head')
- gate_gain_grad: float32 [2048], P('head')
- proj_output_grad: float32 [1024, 2048], P('seq', 'head')
The draws below stay inside these ranges and needn't reach their ends.
Inputs may be any that keep to these rules, and one draw needn't show every extreme that they name: `seq_start`: entry b is a multiple of 256: b * 256 where block b begins a sequence, else entry b - 1. Blocks 0 and 14 begin a sequence, block 15 never does.
All inputs are finite; a program needn't handle non-finite values.
Results may differ from the reference program's by a relative error of at most 0.00065.
The reference program's roundings to bfloat16 on the way (of `normed`, `normed_out` and `cot_half`) count: a program that leaves them out, or rounds other values in their place, can miss the bound.
Values may be sent and summed in bfloat16 or wider, within the bound.
No kernel may reach another device: no remote copies, remote signals or barrier semaphores. Data moves between devices by JAX's collectives and lax.ppermute only.
A program may use at most 192 MiB of HBM per device.

```python
import math
from functools import partial
import jax
import jax.numpy as jnp
from jax import lax

D = 1024
H = 32
N = 128
K = 4
GROUP = 256
TOK_DEV = 256
DI = 2048
BLOCKS = 16
TOKENS = 4096


def draw_decay_log(key, part):
    lowest = math.log(0.2 / TOKENS)
    return jax.random.uniform(key, (H,), jnp.float32, lowest, 0.5)


def draw_seq_start(key, part):
    index = jnp.arange(BLOCKS, dtype=jnp.int32)
    extra = jax.random.randint(jax.random.fold_in(key, 1), (), 1, BLOCKS - 1)
    flags = jax.random.randint(jax.random.fold_in(key, 2), (BLOCKS,), 0, 16) == 0
    flags = flags | (index == 0) | (index == extra) | (index == BLOCKS - 2)
    flags = flags & (index != BLOCKS - 1)
    owner = lax.cummax(jnp.where(flags, index, 0), axis=0)
    return (owner * TOK_DEV).astype(jnp.int32)


def with_spikes(values, stream_key, source, target, blocks, factor):
    def block_of(dim):
        return (jnp.arange(values.shape[dim]) // (values.shape[dim] // blocks)).reshape((-1,) + (1,) * (values.ndim - 1 - dim))

    near = jax.random.permutation(stream_key, blocks)[block_of(target)]
    other_side = (block_of(target) + blocks // 2) % blocks
    return jnp.where((block_of(source) == near) | (block_of(source) == other_side), factor * values, values)


def block_levels(own_key, extent, shards, least, top_value):
    def one(axis_at, blocks):
        draws = jax.random.uniform(jax.random.fold_in(jax.random.fold_in(own_key, 6), axis_at), (blocks,), jnp.float32, least / len(shards), top_value / len(shards))
        return jnp.repeat(jnp.exp(draws), extent[axis_at] // blocks).reshape((-1,) + (1,) * (len(extent) - axis_at - 1))

    loudness = one(*shards[0])
    for cut in shards[1:]:
        loudness = loudness * one(*cut)
    return loudness


def gaussian(own_key, dims, scale, limit, shards=(), held_as=jnp.bfloat16):
    array = scale * jax.random.normal(own_key, dims, jnp.float32)
    if shards:
        array = array * block_levels(own_key, dims, shards, -0.22, 0.18)
    return jnp.clip(array, -limit, limit).astype(held_as)


def bell_draw_with(rng, dims, scale, reach, split, heavy, kind=jnp.bfloat16):
    array = scale * jax.random.normal(rng, dims, jnp.float32)
    if split:
        array = array * block_levels(rng, dims, split, -0.22, 0.18)
    return jnp.clip(with_spikes(array, jax.random.fold_in(rng, 3), *heavy), -reach, reach).astype(kind)


def setup_inputs(seed: int = 0) -> dict:
    seeds = jax.random.split(jax.random.key(seed), 18)
    tokens = bell_draw_with(seeds[0], (TOKENS, D), 1.0, 6.0, ((0, 16),), (0, 1, 16, 2.0), jnp.float32)
    norm_gain = jnp.clip(1.0 + 0.1 * jax.random.normal(seeds[1], (D,), jnp.float32), 0.5, 1.5)
    proj_inner = gaussian(seeds[2], (D, DI), D ** -0.5, 0.1875, ((1, 2),))
    proj_gate = gaussian(seeds[3], (D, DI), D ** -0.5, 0.1875, ((1, 2),))
    proj_step = gaussian(seeds[4], (D, H), D ** -0.5, 0.1875, ((1, 2),))
    proj_state = gaussian(seeds[5], (D, 2 * N), D ** -0.5, 0.1875, ((1, 2),))
    conv_inner = gaussian(seeds[6], (K, DI), K ** -0.5, 3.0, ((1, 2),), jnp.float32)
    conv_state = gaussian(seeds[7], (K, 2 * N), K ** -0.5, 3.0, ((1, 2),), jnp.float32)
    offset_inner = gaussian(seeds[8], (DI,), 0.5, 2.5, ((0, 2),), jnp.float32)
    offset_state = gaussian(seeds[9], (2 * N,), 0.5, 2.5, ((0, 2),), jnp.float32)
    step_bias = jnp.clip(-4.0 + 2.0 * jax.random.uniform(seeds[10], (H,), jnp.float32) ** block_levels(seeds[10], (H,), ((0, 2),), -0.2, 0.2), -4.0, -2.0)
    decay_log = draw_decay_log(jax.random.fold_in(seeds[17], 71), 0)
    skip_gain = jnp.clip(0.5 + 1.0 * jax.random.uniform(seeds[12], (H,), jnp.float32) ** block_levels(seeds[12], (H,), ((0, 2),), -0.2, 0.2), 0.5, 1.5)
    gate_gain = jnp.clip(1.0 + 0.1 * jax.random.normal(seeds[13], (DI,), jnp.float32), 0.5, 1.5)
    proj_output = gaussian(seeds[14], (D, DI), DI ** -0.5, 0.125, ((1, 2),))
    seq_start = draw_seq_start(jax.random.fold_in(seeds[17], 71), 0)
    cotangent = bell_draw_with(seeds[16], (TOKENS, D), 1.0, 6.0, ((0, 16),), (0, 1, 16, 2.0), jnp.float32)
    return dict(tokens=tokens, norm_gain=norm_gain, proj_inner=proj_inner, proj_gate=proj_gate, proj_step=proj_step, proj_state=proj_state, conv_inner=conv_inner, conv_state=conv_state, offset_inner=offset_inner, offset_state=offset_state, step_bias=step_bias, decay_log=decay_log, skip_gain=skip_gain, gate_gain=gate_gain, proj_output=proj_output, seq_start=seq_start, cotangent=cotangent)


EPS = 1e-05
HIGHEST = lax.Precision.HIGHEST

def rms_norm(values, gain):
    scale = lax.rsqrt(lax.optimization_barrier(jnp.mean(values * values, axis=-1, keepdims=True)) + EPS)
    return values * scale * gain

def conv_silu(inputs, border, weight, offset, keep):
    padded = jnp.concatenate([border * keep, inputs], axis=0)
    length = inputs.shape[0]
    taps = weight.shape[0]
    total = offset + weight[taps - 1] * padded[taps - 1:taps - 1 + length]
    for position in range(taps - 1):
        total = total + weight[position] * padded[position:position + length]
    return jax.nn.silu(total)

def step_sizes(step_pre, step_bias, decay_log):
    step = jax.nn.softplus(step_pre + step_bias)
    return (step, -step * jnp.exp(decay_log))

def block_states(inner, writer, step_pre, step_bias, decay_log, span):
    step, log_decay = step_sizes(step_pre, step_bias, decay_log)
    length, heads = step.shape
    count = length // span
    width = inner.shape[1] // heads
    values = inner.reshape(count, span, heads, width)
    cumul = jnp.cumsum(log_decay.reshape(count, span, heads), axis=1)
    factor = jnp.exp(cumul[:, -1:, :] - cumul) * step.reshape(count, span, heads)
    scaled = values * factor[:, :, :, None]
    partial_states = jnp.einsum('cjhp,cjn->chpn', scaled, writer.reshape(count, span, -1), precision=HIGHEST)
    totals = cumul[:, -1, :]
    ending = jnp.zeros_like(partial_states[0])
    for index in range(count):
        ending = jnp.exp(totals[index])[:, None, None] * ending + partial_states[index]
    return (partial_states, ending, lax.optimization_barrier(jnp.sum(totals, axis=0)))

def block_outputs(inner, writer, reader, step_pre, step_bias, decay_log, skip_gain, gate_pre, partial_states, incoming, span):
    step, log_decay = step_sizes(step_pre, step_bias, decay_log)
    length, heads = step.shape
    count = length // span
    width = inner.shape[1] // heads
    values = inner.reshape(count, span, heads, width)
    writers = writer.reshape(count, span, -1)
    readers = reader.reshape(count, span, -1)
    cumul = jnp.cumsum(log_decay.reshape(count, span, heads), axis=1)
    scores = jnp.einsum('cin,cjn->cij', readers, writers, precision=HIGHEST)
    later = lax.broadcasted_iota(jnp.int32, (span, span), 0) >= lax.broadcasted_iota(jnp.int32, (span, span), 1)
    later = later[None, :, :, None]
    spread = cumul[:, :, None, :] - cumul[:, None, :, :]
    decay = jnp.where(later, jnp.exp(jnp.where(later, spread, 0.0)), 0.0)
    weights = scores[:, :, :, None] * decay * step.reshape(count, 1, span, heads)
    result = jnp.einsum('cijh,cjhp->cihp', weights, values, precision=HIGHEST)
    totals = cumul[:, -1, :]
    state = incoming
    starts = []
    for index in range(count):
        starts.append(state)
        state = jnp.exp(totals[index])[:, None, None] * state + partial_states[index]
    before = jnp.stack(starts)
    carried = jnp.einsum('cin,chpn->cihp', readers, before, precision=HIGHEST)
    result = result + jnp.exp(cumul)[:, :, :, None] * carried
    output = result.reshape(length, heads * width) + jnp.repeat(skip_gain, width) * inner
    gated = output * jax.nn.silu(gate_pre)
    return (gated, lax.optimization_barrier(jnp.sum(gated * gated, axis=1)))

def gate_norm(gated, squares, gain, channels):
    return gated * lax.rsqrt(squares[:, None] / channels + EPS) * gain

def reference(tokens, norm_gain, proj_inner, proj_gate, proj_step, proj_state, conv_inner, conv_state, offset_inner, offset_state, step_bias, decay_log, skip_gain, gate_gain, proj_output, seq_start, cotangent):
    inner_width = proj_inner.shape[1]
    state_width = proj_state.shape[1] // 2
    heads = proj_step.shape[1]
    width = inner_width // heads
    count = TOKENS // GROUP
    model = tokens.shape[1]
    conv_weight = jnp.concatenate([conv_inner, conv_state], axis=1)
    conv_offset = jnp.concatenate([offset_inner, offset_state], axis=0)
    lag = conv_weight.shape[0] - 1
    channels = conv_weight.shape[1]
    starts = jnp.arange(count, dtype=jnp.int32) * GROUP
    owners = (starts // TOK_DEV).astype(jnp.int32)
    keeps = 1.0 - (seq_start[owners] == starts).astype(jnp.float32)
    blocks = tokens.reshape(count, GROUP, model)
    cot_blocks = cotangent.reshape(count, GROUP, model)
    rowwise = (((1,), (1,)), ((), ()))
    over_rows = (((0,), (0,)), ((), ()))

    def project(block):
        normed = rms_norm(block, norm_gain).astype(jnp.bfloat16)
        inner_pre = jnp.dot(normed, proj_inner, preferred_element_type=jnp.float32)
        state_pre = jnp.dot(normed, proj_state, preferred_element_type=jnp.float32)
        gate_pre = jnp.dot(normed, proj_gate, preferred_element_type=jnp.float32)
        step_pre = jnp.dot(normed, proj_step, preferred_element_type=jnp.float32)
        return (normed, jnp.concatenate([inner_pre, state_pre], axis=1), gate_pre, step_pre)

    def mixer(pre_all, gate_pre, step_pre, border, entering, weight, offset, bias, decay, skip, gain, keep):
        mixed = conv_silu(pre_all, border, weight, offset, keep)
        inner = mixed[:, :inner_width]
        writer = mixed[:, inner_width:inner_width + state_width]
        reader = mixed[:, inner_width + state_width:]
        incoming = keep * entering
        partial_states, ending, total = block_states(inner, writer, step_pre, bias, decay, GROUP)
        gated, squares = block_outputs(inner, writer, reader, step_pre, bias, decay, skip, gate_pre, partial_states, incoming, GROUP)
        normed_out = gate_norm(gated, squares, gain, float(inner_width))
        leaving = jnp.exp(total)[:, None, None] * incoming + ending
        return (normed_out, leaving, pre_all[pre_all.shape[0] - lag:])

    def forward(carry, inputs):
        entering, border = carry
        block, keep = inputs
        normed, pre_all, gate_pre, step_pre = project(block)
        normed_out, leaving, edge = mixer(pre_all, gate_pre, step_pre, border, entering, conv_weight, conv_offset, step_bias, decay_log, skip_gain, gate_gain, keep)
        branch = lax.dot_general(normed_out.astype(jnp.bfloat16), proj_output, rowwise, preferred_element_type=jnp.float32)
        return ((leaving, edge), (block + branch, entering, border))
    start = (jnp.zeros((heads, width, state_width), jnp.float32), jnp.zeros((lag, channels), jnp.float32))
    _, (outputs, enterings, borders) = lax.scan(forward, start, (blocks, keeps))

    def backward(carry, inputs):
        state_grad, border_grad, sums = carry
        block, cot_block, keep, entering, border = inputs
        normed, pre_all, gate_pre, step_pre = project(block)
        local = partial(mixer, keep=keep)
        (normed_out, _, _), pullback = jax.vjp(local, pre_all, gate_pre, step_pre, border, entering, conv_weight, conv_offset, step_bias, decay_log, skip_gain, gate_gain)
        cot_half = cot_block.astype(jnp.bfloat16)
        out_half = normed_out.astype(jnp.bfloat16)
        out_cot = jnp.dot(cot_half, proj_output, preferred_element_type=jnp.float32)
        grads = pullback((out_cot, state_grad, border_grad))
        pre_half = grads[0].astype(jnp.bfloat16)
        gate_half = grads[1].astype(jnp.bfloat16)
        step_half = grads[2].astype(jnp.bfloat16)
        inner_half = pre_half[:, :inner_width]
        state_half = pre_half[:, inner_width:]
        normed_grad = lax.dot_general(inner_half, proj_inner, rowwise, preferred_element_type=jnp.float32)
        normed_grad = normed_grad + lax.dot_general(gate_half, proj_gate, rowwise, preferred_element_type=jnp.float32)
        normed_grad = normed_grad + lax.dot_general(step_half, proj_step, rowwise, preferred_element_type=jnp.float32)
        normed_grad = normed_grad + lax.dot_general(state_half, proj_state, rowwise, preferred_element_type=jnp.float32)
        _, norm_pull = jax.vjp(rms_norm, block, norm_gain)
        token_grad, gain_grad = norm_pull(normed_grad)
        terms = (gain_grad, lax.dot_general(normed, inner_half, over_rows, preferred_element_type=jnp.float32), lax.dot_general(normed, gate_half, over_rows, preferred_element_type=jnp.float32), lax.dot_general(normed, step_half, over_rows, preferred_element_type=jnp.float32), lax.dot_general(normed, state_half, over_rows, preferred_element_type=jnp.float32), grads[5], grads[6], grads[7], grads[8], grads[9], grads[10], lax.dot_general(cot_half, out_half, over_rows, preferred_element_type=jnp.float32))
        sums = tuple((old + new for old, new in zip(sums, terms)))
        return ((grads[4], grads[3], sums), cot_block + token_grad)
    zeros = (jnp.zeros((model,), jnp.float32), jnp.zeros(proj_inner.shape, jnp.float32), jnp.zeros(proj_gate.shape, jnp.float32), jnp.zeros(proj_step.shape, jnp.float32), jnp.zeros(proj_state.shape, jnp.float32), jnp.zeros(conv_weight.shape, jnp.float32), jnp.zeros(conv_offset.shape, jnp.float32), jnp.zeros(step_bias.shape, jnp.float32), jnp.zeros(decay_log.shape, jnp.float32), jnp.zeros(skip_gain.shape, jnp.float32), jnp.zeros(gate_gain.shape, jnp.float32), jnp.zeros(proj_output.shape, jnp.float32))
    begin = (jnp.zeros((heads, width, state_width), jnp.float32), jnp.zeros((lag, channels), jnp.float32), zeros)
    (_, _, sums), input_blocks = lax.scan(backward, begin, (blocks, cot_blocks, keeps, enterings, borders), reverse=True)
    block_output = outputs.reshape(TOKENS, model)
    input_grad = input_blocks.reshape(TOKENS, model)
    return (block_output, input_grad, sums[0], sums[1], sums[2], sums[3], sums[4], sums[5][:, :inner_width], sums[5][:, inner_width:], sums[6][:inner_width], sums[6][inner_width:], sums[7], sums[8], sums[9], sums[10], sums[11])
```

```python
import jax
import jax.numpy as jnp
from jax import lax
from jax.sharding import PartitionSpec as P

EPS = 1e-05
HIGHEST = lax.Precision.HIGHEST
ROWWISE = (((1,), (1,)), ((), ()))
OVER_ROWS = (((0,), (0,)), ((), ()))
F32 = jnp.float32
BF16 = jnp.bfloat16
HALO = 8


def shift(array, by):
    length = lax.axis_size("seq")
    pairs = [(i, i + by) for i in range(length) if 0 <= i + by < length]
    return lax.ppermute(array, "seq", pairs)


def swap(array, bit):
    return lax.ppermute(array, "seq", [(i, i ^ bit) for i in range(lax.axis_size("seq"))])


def swap_head(array):
    return lax.ppermute(array, "head", [(0, 1), (1, 0)])


def dot(a, b, dims=(((1,), (0,)), ((), ()))):
    return lax.dot_general(a, b, dims, preferred_element_type=F32)


def exact(a, b, dims=(((1,), (0,)), ((), ()))):
    return lax.dot_general(a, b, dims, precision=HIGHEST, preferred_element_type=F32)


def norm_rows(values, gain):
    scale = lax.rsqrt(jnp.mean(values * values, axis=-1, keepdims=True) + EPS)
    return (values * scale * gain).astype(BF16)


def silu_slope(x):
    sig = jax.nn.sigmoid(x)
    return sig * (1.0 + x * (1.0 - sig))


def fold(parts, factors, reverse):
    count = parts.shape[0]
    state = jnp.zeros_like(parts[0])
    outs = [None] * count
    for turn in range(count):
        source = count - 1 - turn if reverse else turn
        outs[source] = state
        state = state * factors[source] + parts[source]
    return jnp.stack(outs)


def spread_rows(array, seq, bits):
    rows, cols = array.shape
    blocks = array.reshape(rows, seq // 4, 2, 2, cols // seq)
    return blocks.transpose(0, 3, 2, 1, 4).reshape(rows, cols)


def pick(array, index, size):
    return lax.dynamic_slice_in_dim(array, index * size, size, axis=0)


def scatter_sum(mine, others, acts, acts_other, place, seq):
    grad = dot(jnp.concatenate([mine, others], 0), jnp.concatenate([acts, acts_other], 0), OVER_ROWS)
    half = grad.shape[0] // 2
    bit = (place // 2) % 2
    grad = pick(grad, bit, half) + swap(pick(grad, 1 - bit, half), 2)
    rest = seq // 4
    group = place // 4
    size = half // rest
    total = pick(grad, group, size)
    for other in range(1, rest):
        total = total + swap(pick(grad, group ^ other, size), 4 * other)
    return total


def per_device(
    tokens,
    norm_gain,
    proj_inner,
    proj_gate,
    proj_step,
    proj_state,
    conv_inner,
    conv_state,
    offset_inner,
    offset_state,
    step_bias,
    decay_log,
    skip_gain,
    gate_gain,
    proj_output,
    seq_start,
    cotangent,
):
    seq = lax.axis_size("seq")
    place = lax.axis_index("seq")
    head = lax.axis_index("head")
    length, model = tokens.shape
    wide = proj_inner.shape[1]
    heads = proj_step.shape[1]
    width = wide // heads
    lag = conv_inner.shape[0] - 1
    keep = 1.0 - (seq_start[0] == place * length).astype(F32)

    tail = shift(tokens[length - HALO :], 1)
    keep_next = shift(jnp.full((8, 128), keep, F32), -1)[0, 0]
    proj_state_other = swap_head(proj_state)
    small_other = swap_head(jnp.concatenate([conv_state, offset_state[None]], 0))
    cot_half = cotangent.astype(BF16)

    normed = norm_rows(tokens, norm_gain)
    normed_tail = norm_rows(tail, norm_gain)
    low = place % 2
    halves = model // 2
    nperm = spread_rows(normed, seq, None)
    cperm = spread_rows(cot_half, seq, None)
    take = lambda a, b: lax.dynamic_slice_in_dim(a, b * halves, halves, axis=1)
    n_mine, c_mine = take(nperm, low), take(cperm, low)
    n_other = swap(take(nperm, 1 - low), 1)
    c_other = swap(take(cperm, 1 - low), 1)

    both = jnp.concatenate([normed_tail, normed], 0)
    border_rows = jnp.where(jnp.arange(length + HALO)[:, None] < HALO, keep, 1.0)

    def conv(pre, weight, offset):
        padded = pre * border_rows
        total = offset + weight[lag] * padded[HALO:]
        for k in range(lag):
            total = total + weight[k] * padded[HALO - lag + k : HALO - lag + k + length]
        return total, padded

    inner_tot, inner_pad = conv(dot(both, proj_inner), conv_inner, offset_inner)
    own_tot, own_pad = conv(dot(both, proj_state), conv_state, offset_state)
    other_tot, _ = conv(dot(both, proj_state_other), small_other[: lag + 1], small_other[lag + 1])
    gate_pre = dot(normed, proj_gate)
    step_pre = dot(normed, proj_step)
    x = jax.nn.silu(inner_tot)
    own = jax.nn.silu(own_tot)
    other = jax.nn.silu(other_tot)
    writer = jnp.where(head == 0, own, other)
    reader = jnp.where(head == 0, other, own)

    z = step_pre + step_bias
    step = jax.nn.softplus(z)
    rate = jnp.exp(decay_log)
    log_decay = -step * rate
    a = jnp.cumsum(log_decay, axis=0)
    total = a[length - 1]
    chan = lambda v: jnp.repeat(v, width, axis=-1)
    per_head = lambda v: jnp.sum(v.reshape(length, heads, width), axis=-1)
    left = jnp.exp(total - a)
    f = left * step
    scaled = x * chan(f)
    states = exact(scaled, writer, OVER_ROWS)

    rows = wide // seq
    group = rows // 8
    passing = jnp.exp(total) * keep
    factor_rows = jnp.broadcast_to(chan(passing).reshape(seq, 8, group)[:, :, :1], (seq, 8, writer.shape[1]))
    sent = jnp.concatenate([states.reshape(seq, rows, -1), factor_rows], 1)
    got = lax.all_to_all(sent, "seq", 0, 0, tiled=True)
    factors = jnp.repeat(got[:, rows:], group, axis=1)
    before = fold(got[:, :rows], factors, False)
    incoming = keep * lax.all_to_all(before, "seq", 0, 0, tiled=True).reshape(wide, -1)

    ti = lax.broadcasted_iota(jnp.int32, (length, length), 0)
    tj = lax.broadcasted_iota(jnp.int32, (length, length), 1)
    scores = exact(reader, writer, ROWWISE)
    later = (ti >= tj)[:, :, None]
    spread = a[:, None, :] - a[None, :, :]
    decay = jnp.where(later, jnp.exp(jnp.where(later, spread, 0.0)), 0.0)
    xs = x * chan(step)
    xs3 = xs.reshape(length, heads, width)
    weights = scores[:, :, None] * decay
    y_in = jnp.einsum("ijh,jhp->ihp", weights, xs3, precision=HIGHEST).reshape(length, wide)

    out_cot = dot(cot_half, proj_output)
    ea = chan(jnp.exp(a))
    carried = exact(reader, incoming, ROWWISE)
    skip = chan(skip_gain)
    output = y_in + ea * carried + skip * x
    sig = jax.nn.sigmoid(gate_pre)
    silu_g = gate_pre * sig
    gated = output * silu_g
    og = out_cot * gate_gain
    sums = jnp.stack([jnp.sum(gated * gated, axis=1), jnp.sum(og * gated, axis=1)])
    sums = sums + swap_head(sums)
    channels = float(wide * lax.axis_size("head"))
    r = lax.rsqrt(sums[0] / channels + EPS)[:, None]
    scaled_gated = gated * r
    out_half = (scaled_gated * gate_gain).astype(BF16)
    gate_gain_grad = jnp.sum(out_cot * scaled_gated, axis=0)
    dgated = og * r - gated * (sums[1][:, None] * r * r * r / channels)
    dout = dgated * silu_g
    gate_half = (dgated * output * silu_slope(gate_pre)).astype(BF16)
    dc = ea * dout
    dstate = exact(dc, reader, OVER_ROWS)
    back = lax.all_to_all((keep * dstate).reshape(seq, rows, -1), "seq", 0, 0, tiled=True)
    after = fold(back, factors, True)
    ending = lax.all_to_all(after, "seq", 0, 0, tiled=True).reshape(wide, -1)

    branch = dot(out_half, proj_output, ROWWISE)
    block_output = tokens + (branch + swap_head(branch))
    output_grad = scatter_sum(c_mine, c_other, out_half, swap(out_half, 1), place, seq)
    gate_grad = scatter_sum(n_mine, n_other, gate_half, swap(gate_half, 1), place, seq)
    skip_grad = jnp.sum(per_head(dout * x), axis=0)
    dout3 = dout.reshape(length, heads, width)
    dxs = jnp.einsum("ijh,ihp->jhp", weights, dout3, precision=HIGHEST).reshape(length, wide)
    dscores = jnp.sum(jnp.einsum("ihp,jhp->ijh", dout3, xs3, precision=HIGHEST) * decay, axis=2)
    dreader = exact(dc, incoming) + exact(dscores, writer)
    dwriter = exact(dscores, reader, OVER_ROWS)
    ds = per_head(x * dxs)
    da = per_head(dout * y_in + dc * carried) - step * ds
    dx = skip * dout + chan(step) * dxs

    dscaled = exact(writer, ending, ROWWISE)
    dwriter = dwriter + exact(scaled, ending)
    q = per_head(x * dscaled)
    dx = dx + chan(f) * dscaled
    ds = ds + left * q
    fq = f * q
    last = jnp.sum(fq, axis=0) + jnp.exp(total) * jnp.sum((incoming * ending).reshape(heads, -1), axis=1)
    da = da - fq
    da = jnp.concatenate([da[: length - 1], da[length - 1 :] + last], 0)
    dlog = jnp.cumsum(da[::-1], axis=0)[::-1]
    ds = ds - rate * dlog
    decay_grad = jnp.sum(dlog * log_decay, axis=0)
    dz = ds * jax.nn.sigmoid(z)
    bias_grad = jnp.sum(dz, axis=0)
    step_half = dz.astype(BF16)

    send = jnp.where(head == 0, dreader, dwriter)
    stay = jnp.where(head == 0, dwriter, dreader)
    down = stay + swap_head(send)
    inner_dt = dx * silu_slope(inner_tot)
    own_dt = down * silu_slope(own_tot)
    dtot = jnp.concatenate([inner_dt, own_dt], 1)
    ahead = shift(dtot[:HALO], -1) * keep_next
    extended = jnp.concatenate([dtot, ahead], 0)
    conv_weight = jnp.concatenate([conv_inner, conv_state], 1)
    pre_grad = conv_weight[lag] * dtot
    for k in range(lag):
        pre_grad = pre_grad + conv_weight[k] * extended[lag - k : lag - k + length]
    padded = jnp.concatenate([inner_pad, own_pad], 1)
    weight_grad = jnp.stack(
        [jnp.sum(dtot * padded[HALO - lag + k : HALO - lag + k + length], axis=0) for k in range(lag + 1)]
    )
    offset_grad = jnp.sum(dtot, axis=0)
    pre_half = pre_grad.astype(BF16)
    inner_half = pre_half[:, :wide]
    state_half = pre_half[:, wide:]
    acts = jnp.concatenate([pre_half, step_half, jnp.zeros((length, 128 - heads), BF16)], 1)
    last_grad = scatter_sum(n_mine, n_other, acts, swap(acts, 1), place, seq)

    normed_grad = dot(inner_half, proj_inner, ROWWISE)
    normed_grad = normed_grad + dot(gate_half, proj_gate, ROWWISE)
    normed_grad = normed_grad + dot(step_half, proj_step, ROWWISE)
    normed_grad = normed_grad + dot(state_half, proj_state, ROWWISE)
    normed_grad = normed_grad + swap_head(normed_grad)
    scale = lax.rsqrt(jnp.mean(tokens * tokens, axis=-1, keepdims=True) + EPS)
    gained = normed_grad * norm_gain
    dot_rows = jnp.sum(gained * tokens, axis=-1, keepdims=True)
    input_grad = cotangent + (gained * scale - tokens * (scale * scale * scale * dot_rows / model))
    norm_gain_grad = jnp.sum(normed_grad * (tokens * scale), axis=0)

    cols = acts.shape[1]
    line = lambda v: jnp.pad(v, (0, cols - v.shape[0]))[None]
    small = jnp.concatenate(
        [
            jnp.pad(weight_grad, ((0, 0), (0, cols - weight_grad.shape[1]))),
            line(offset_grad),
            line(gate_gain_grad),
            line(jnp.concatenate([bias_grad, decay_grad, skip_grad])),
            line(norm_gain_grad),
        ],
        0,
    )
    bit = 1
    while bit < seq:
        small = small + swap(small, bit)
        bit *= 2
    taps = lag + 1
    vec = small[taps + 2]
    gain_part = lax.dynamic_slice_in_dim(small[taps + 3], place * (model // seq), model // seq)
    mixed = wide + state_half.shape[1]
    return (
        block_output,
        input_grad,
        gain_part,
        last_grad[:, :wide],
        gate_grad,
        last_grad[:, mixed : mixed + heads],
        last_grad[:, wide:mixed],
        small[:taps, :wide],
        small[:taps, wide:mixed],
        small[taps, :wide],
        small[taps, wide:mixed],
        vec[:heads],
        vec[heads : 2 * heads],
        vec[2 * heads : 3 * heads],
        small[taps + 1, :wide],
        output_grad,
    )


def solution(mesh):
    placed = (
        P("seq", None),
        P(),
        P(None, "head"),
        P(None, "head"),
        P(None, "head"),
        P(None, "head"),
        P(None, "head"),
        P(None, "head"),
        P("head"),
        P("head"),
        P("head"),
        P("head"),
        P("head"),
        P("head"),
        P(None, "head"),
        P("seq"),
        P("seq", None),
    )
    return jax.shard_map(
        per_device,
        mesh=mesh,
        in_specs=placed,
        out_specs=(
            P("seq", None),
            P("seq", None),
            P("seq"),
            P("seq", "head"),
            P("seq", "head"),
            P("seq", "head"),
            P("seq", "head"),
            P(None, "head"),
            P(None, "head"),
            P("head"),
            P("head"),
            P("head"),
            P("head"),
            P("head"),
            P("head"),
            P("seq", "head"),
        ),
        check_vma=False,
    )
```
